32 devices in a mesh: loss: 4 (over x, core), tower: 4 (over z), pipe: 2 (over y).
Axes of the slice: x: 2, y: 2, z: 4, core: 2. Of those that a mesh axis runs over, the one named last changes fastest.
Arguments:
- image_feats: bfloat16 [4, 2, 24, 1536], P('loss', 'pipe', None, 'tower'), may hold values from -6 to 6
- text_tokens: bfloat16 [4, 2, 24, 64, 1152], P('loss', 'pipe', None, None, 'tower'), may hold values from -6 to 6
- lengths: int32 [4, 2, 24], P('loss', 'pipe'), may hold values from 1 to 64, as said below
- w_image: bfloat16 [1536, 1536], P('tower'), may hold values from -0.15625 to 0.15625
- w_text: bfloat16 [1152, 1536], P('tower'), may hold values from -0.1875 to 0.1875
- logit_scale: float32 [1], replicated, may hold values from 24 to 48
- logit_bias: float32 [1], replicated, may hold values from -4 to -2
Outputs:
- image_grad: float32 [4, 2, 24, 1536], P('loss', 'pipe', 'tower')
- text_grad: float32 [4, 2, 24, 1536], P('loss', 'pipe', 'tower')
The draws below stay inside these ranges and needn't reach their ends.
Inputs may be any that keep to these rules, and one draw needn't show every extreme that they name: `lengths`: in every group of 24 captions one caption has 64 tokens and one has a single token.
All inputs are finite; a program needn't handle non-finite values.
Results may differ from the reference program's by a relative error of at most 0.0036.
The reference program's roundings to bfloat16 on the way count: a program that leaves them out, or rounds other values in their place, can miss the bound.
Values may be sent and summed in bfloat16 or wider, within the bound.
A program may use at most 64 MiB of HBM per device.

```python
import math
import jax
import jax.numpy as jnp
from jax import lax

IMG_WIDTH = 1536
TEXT_WIDTH = 1152
EMB = 1536
TEXT_LEN = 64
GROUP = 24
N_LOSS = 4
N_PIPE = 2


def draw_lengths(key, part):
    values = jax.random.randint(key, (N_LOSS, N_PIPE, GROUP), 1, TEXT_LEN + 1, dtype=jnp.int32)
    values = values.at[:, :, 0].set(TEXT_LEN)
    return values.at[:, :, 1].set(1)


def levels(rng, dims, shards, low, top_value):
    level = 1.0
    for position, parts in shards:
        heights = jax.random.uniform(jax.random.fold_in(jax.random.fold_in(rng, 6), position), (parts,), jnp.float32, low / len(shards), top_value / len(shards))
        level = level * jnp.repeat(jnp.exp(heights), dims[position] // parts).reshape((-1,) + (1,) * (len(dims) - 1 - position))
    return level


def normal_values(key, shape, width, bound, shards=(), kind=jnp.bfloat16):
    gain = levels(key, shape, shards, -0.22, 0.18) if shards else 1.0
    drawn = jax.random.normal(key, shape, jnp.float32) * width * gain
    return jnp.minimum(jnp.maximum(drawn, -bound), bound).astype(kind)


def setup_inputs(seed: int = 0) -> dict:
    key_list = jax.random.split(jax.random.key(seed), 8)
    return {
        "image_feats": normal_values(key_list[0], (N_LOSS, N_PIPE, GROUP, IMG_WIDTH), 1.0, 6.0, ((0, 4), (1, 2), (3, 4))),
        "text_tokens": normal_values(key_list[1], (N_LOSS, N_PIPE, GROUP, TEXT_LEN, TEXT_WIDTH), 1.0, 6.0, ((0, 4), (1, 2), (4, 4))),
        "lengths": draw_lengths(jax.random.fold_in(key_list[7], 71), 0),
        "w_image": normal_values(key_list[3], (IMG_WIDTH, EMB), IMG_WIDTH ** -0.5, 0.15625, ((0, 4),)),
        "w_text": normal_values(key_list[4], (TEXT_WIDTH, EMB), TEXT_WIDTH ** -0.5, 0.1875, ((0, 4),)),
        "logit_scale": jnp.clip(jnp.exp(jax.random.uniform(key_list[5], (1,), jnp.float32, math.log(24.0), math.log(48.0))), 24.0, 48.0),
        "logit_bias": jnp.clip(jax.random.uniform(key_list[6], (1,), jnp.float32, -4.0, -2.0), -4.0, -2.0),
    }


def normalize(raw):
    return raw * lax.rsqrt(lax.optimization_barrier(jnp.sum(raw * raw, axis=-1, keepdims=True)) + 1e-06)

def reference(image_feats, text_tokens, lengths, w_image, w_text, logit_scale, logit_bias):
    batch = N_LOSS * N_PIPE * GROUP
    images = image_feats.reshape(batch, IMG_WIDTH)
    image_unit = normalize(jnp.dot(images, w_image, preferred_element_type=jnp.float32)).astype(jnp.bfloat16)
    places = jnp.arange(TEXT_LEN, dtype=jnp.int32)[None, :]

    def pool(block):
        words, counts = block
        keep = (places < counts[:, None]).astype(jnp.float32)
        summed = jnp.einsum('bl,bld->bd', keep, words.astype(jnp.float32))
        return (summed / counts.astype(jnp.float32)[:, None]).astype(jnp.bfloat16)
    pooled = lax.map(pool, (text_tokens.reshape(batch // GROUP, GROUP, TEXT_LEN, TEXT_WIDTH), lengths.reshape(batch // GROUP, GROUP))).reshape(batch, TEXT_WIDTH)
    text_unit = normalize(jnp.dot(pooled, w_text, preferred_element_type=jnp.float32)).astype(jnp.bfloat16)
    scale = logit_scale[0]
    shift = logit_bias[0]
    text_ids = jnp.arange(batch, dtype=jnp.int32)

    def step(carry, block):
        rows, row_ids = block
        scores = jnp.dot(rows, text_unit.T, preferred_element_type=jnp.float32)
        match = (row_ids[:, None] == text_ids[None, :]).astype(jnp.float32)
        grads = (jax.nn.sigmoid(scale * scores + shift) - match).astype(jnp.bfloat16)
        image_part = scale * jnp.dot(grads, text_unit, preferred_element_type=jnp.float32)
        carry = carry + scale * jnp.dot(grads.T, rows, preferred_element_type=jnp.float32)
        return (carry, image_part)
    start = jnp.zeros((batch, EMB), jnp.float32)
    text_grad, image_parts = lax.scan(step, start, (image_unit.reshape(batch // GROUP, GROUP, EMB), text_ids.reshape(batch // GROUP, GROUP)))
    image_grad = image_parts.reshape(N_LOSS, N_PIPE, GROUP, EMB)
    return (image_grad, text_grad.reshape(N_LOSS, N_PIPE, GROUP, EMB))
```

```python
import functools

import jax
import jax.numpy as jnp
from jax import lax
from jax.experimental import pallas as pl
from jax.experimental.pallas import tpu as pltpu
from jax.sharding import PartitionSpec as P

MESH = pl.DeviceIdType.MESH
WIRE = jnp.bfloat16
SUM = jnp.float32
F32 = jnp.float32
UNROLL = 16


def each(lo, hi, body):
    if hi - lo <= UNROLL:
        for k in range(lo, hi):
            body(k)
    else:
        lax.fori_loop(lo, hi, lambda k, c: (body(k), c)[1], 0)


def kernel(
    sub, towers, pipes, planes,
    scale_ref, shift_ref, feats_hbm, words_hbm, lens_hbm, wi_hbm, wt_hbm,
    image_out, text_out,
    feats, words, lens, wi, wt,
    part_i, part_t, got_i, got_t, images, texts, term_i, term_t, back_i, back_t,
    load_sem, s1, r1, s2, r2, s3, r3, s4, r4, s5, r5, s6, r6,
):
    pad = images.shape[1]
    group, width = feats.shape
    length = words.shape[1]
    emb = wi.shape[1]
    rows = towers * pad
    tower = lax.axis_index("tower")
    plane = lax.axis_index("loss") * pipes + lax.axis_index("pipe")

    def tower_peer(k):
        return {"tower": lax.rem(tower + k, towers)}

    def plane_peer(k):
        q = lax.rem(plane + k, planes)
        return {"loss": q // pipes, "pipe": lax.rem(q, pipes)}

    loads = []
    for n, (src, dst) in enumerate((
        (lens_hbm.at[0], lens),
        (words_hbm.at[0, 0], words),
        (wt_hbm, wt),
        (feats_hbm.at[0, 0], feats),
        (wi_hbm, wi),
    )):
        loads.append(pltpu.make_async_copy(src, dst, load_sem.at[n]))
        loads[-1].start()

    barrier = pltpu.get_barrier_semaphore()
    each(1, towers, lambda k: pl.semaphore_signal(
        barrier, inc=1, device_id=tower_peer(k), device_id_type=MESH))
    each(1, planes, lambda k: pl.semaphore_signal(
        barrier, inc=1, device_id=plane_peer(k), device_id_type=MESH))

    def source_row(shape):
        at = lax.broadcasted_iota(jnp.int32, shape, 0)
        r = at % pad
        return jnp.where(r < sub, at // pad * sub + r, -1)

    pick = (source_row((rows, group)) == lax.broadcasted_iota(jnp.int32, (rows, group), 1))

    def scatter(k, part, got, send, recv):
        return pltpu.make_async_remote_copy(
            src_ref=part.at[lax.rem(tower + k, towers)], dst_ref=got.at[k - 1],
            send_sem=send.at[k - 1], recv_sem=recv.at[k - 1],
            device_id=tower_peer(k), device_id_type=MESH)

    loads[0].wait()
    counts = jnp.sum(jnp.where(pick, lens[...].astype(F32), 0.0), axis=1, keepdims=True)
    spot = lax.broadcasted_iota(jnp.int32, (rows, group * length), 1)
    first = source_row((rows, group * length)) * length
    keep = (spot >= first) & (spot < first + counts.astype(jnp.int32)) & (first >= 0)
    keep = jnp.where(keep, 1.0, 0.0).astype(jnp.bfloat16)
    loads[1].wait()
    summed = jnp.dot(keep, words[...].reshape(group * length, words.shape[2]),
                     preferred_element_type=F32)
    pooled = (summed / jnp.maximum(counts, 1.0)).astype(jnp.bfloat16)
    loads[2].wait()
    raw_t = jnp.dot(pooled, wt[...], preferred_element_type=F32).reshape(towers, pad, emb)
    part_t[...] = raw_t
    pl.semaphore_wait(barrier, towers + planes - 2)
    each(1, towers, lambda k: scatter(k, part_t, got_t, s1, r1).start())

    loads[3].wait()
    moved = jnp.dot(jnp.where(pick, 1.0, 0.0).astype(jnp.bfloat16), feats[...],
                    preferred_element_type=F32).astype(jnp.bfloat16)
    loads[4].wait()
    raw_i = jnp.dot(moved, wi[...], preferred_element_type=F32).reshape(towers, pad, emb)
    part_i[...] = raw_i
    each(1, towers, lambda k: scatter(k, part_i, got_i, s2, r2).start())

    def unit(part, got, send, recv):
        each(1, towers, lambda k: scatter(k, part, got, send, recv).wait_recv())
        raw = part[tower]
        for k in range(towers - 1):
            raw = raw + got[k]
        size = jnp.sum(raw * raw, axis=-1, keepdims=True) + 1e-06
        return (raw * lax.rsqrt(size)).astype(jnp.bfloat16)

    def spread_t(k):
        return pltpu.make_async_remote_copy(
            src_ref=texts.at[plane], dst_ref=texts.at[plane],
            send_sem=s3.at[k - 1], recv_sem=r3.at[k - 1],
            device_id=plane_peer(k), device_id_type=MESH)

    def spread_i(k):
        return pltpu.make_async_remote_copy(
            src_ref=images.at[tower], dst_ref=images.at[tower],
            send_sem=s4.at[k - 1], recv_sem=r4.at[k - 1],
            device_id=tower_peer(k), device_id_type=MESH)

    texts[plane] = unit(part_t, got_t, s1, r1)
    each(1, planes, lambda k: spread_t(k).start())
    images[tower] = unit(part_i, got_i, s2, r2)
    each(1, towers, lambda k: spread_i(k).start())
    each(1, planes, lambda k: spread_t(k).wait_recv())
    each(1, towers, lambda k: spread_i(k).wait_recv())

    scale = scale_ref[0]
    shift = shift_ref[0]
    cols = planes * pad
    all_i = images[...].astype(F32).reshape(rows, emb).astype(jnp.bfloat16)
    all_t = texts[...].astype(F32).reshape(cols, emb).astype(jnp.bfloat16)
    scores = lax.dot_general(all_i, all_t, (((1,), (1,)), ((), ())), preferred_element_type=F32)
    at_i = lax.broadcasted_iota(jnp.int32, (rows, cols), 0) - tower * pad
    at_t = lax.broadcasted_iota(jnp.int32, (rows, cols), 1) - plane * pad
    match = jnp.where((at_i == at_t) & (at_i >= 0) & (at_i < pad), 1.0, 0.0)
    grads = jax.nn.sigmoid(scale * scores + shift) - match

    def back_image(k):
        return pltpu.make_async_remote_copy(
            src_ref=term_i.at[lax.rem(tower + k, towers)], dst_ref=back_i.at[k - 1],
            send_sem=s5.at[k - 1], recv_sem=r5.at[k - 1],
            device_id=tower_peer(k), device_id_type=MESH)

    def back_text(k):
        return pltpu.make_async_remote_copy(
            src_ref=term_t.at[lax.rem(plane + k, planes)], dst_ref=back_t.at[k - 1],
            send_sem=s6.at[k - 1], recv_sem=r6.at[k - 1],
            device_id=plane_peer(k), device_id_type=MESH)

    grads_t = grads.T.astype(jnp.bfloat16)
    sums_t = jnp.dot(grads_t, all_i, preferred_element_type=F32)
    term_t[...] = sums_t.reshape(planes, pad, emb).astype(WIRE)
    each(1, planes, lambda k: back_text(k).start())
    sums_i = jnp.dot(grads.astype(jnp.bfloat16), all_t, preferred_element_type=F32)
    term_i[...] = sums_i.reshape(towers, pad, emb).astype(WIRE)
    each(1, towers, lambda k: back_image(k).start())

    mine_t = lax.broadcasted_iota(jnp.int32, (pad, cols), 0) + plane * pad
    mine_t = jnp.where(mine_t == lax.broadcasted_iota(jnp.int32, (pad, cols), 1), 1.0, 0.0)
    mine_i = lax.broadcasted_iota(jnp.int32, (pad, rows), 0) + tower * pad
    mine_i = jnp.where(mine_i == lax.broadcasted_iota(jnp.int32, (pad, rows), 1), 1.0, 0.0)
    own_gt = jnp.dot(mine_t.astype(jnp.bfloat16), grads_t, preferred_element_type=F32)
    own_gi = jnp.dot(mine_i.astype(jnp.bfloat16), grads.astype(jnp.bfloat16),
                     preferred_element_type=F32)
    own_t = jnp.dot(own_gt.astype(jnp.bfloat16), all_i, preferred_element_type=F32)
    own_i = jnp.dot(own_gi.astype(jnp.bfloat16), all_t, preferred_element_type=F32)

    each(1, planes, lambda k: back_text(k).wait_recv())
    text_out[0, 0] = (scale * (own_t + jnp.sum(back_t[...].astype(F32), axis=0)))[:sub]
    each(1, towers, lambda k: back_image(k).wait_recv())
    image_out[0, 0] = (scale * (own_i + jnp.sum(back_i[...].astype(F32), axis=0)))[:sub]

    each(1, towers, lambda k: scatter(k, part_t, got_t, s1, r1).wait_send())
    each(1, towers, lambda k: scatter(k, part_i, got_i, s2, r2).wait_send())
    each(1, planes, lambda k: spread_t(k).wait_send())
    each(1, towers, lambda k: spread_i(k).wait_send())
    each(1, towers, lambda k: back_image(k).wait_send())
    each(1, planes, lambda k: back_text(k).wait_send())


def per_device(towers, pipes, planes, image_feats, text_tokens, lengths, w_image, w_text,
               logit_scale, logit_bias):
    group = image_feats.shape[2]
    emb = w_image.shape[1]
    sub = group // towers
    pad = -(-sub // 8) * 8
    out = jax.ShapeDtypeStruct((1, 1, sub, emb), F32)
    sems = []
    for n in (towers, towers, planes, towers, towers, planes):
        sems += [pltpu.SemaphoreType.DMA((n - 1,))] * 2
    return pl.pallas_call(
        functools.partial(kernel, sub, towers, pipes, planes),
        out_shape=(out, out),
        in_specs=[pl.BlockSpec(memory_space=pltpu.SMEM)] * 2
        + [pl.BlockSpec(memory_space=pl.ANY)] * 5,
        out_specs=(pl.BlockSpec(memory_space=pltpu.VMEM),) * 2,
        scratch_shapes=[
            pltpu.VMEM(image_feats.shape[2:], image_feats.dtype),
            pltpu.VMEM(text_tokens.shape[2:], text_tokens.dtype),
            pltpu.VMEM(lengths.shape[1:], lengths.dtype),
            pltpu.VMEM(w_image.shape, w_image.dtype),
            pltpu.VMEM(w_text.shape, w_text.dtype),
            pltpu.VMEM((towers, pad, emb), SUM),
            pltpu.VMEM((towers, pad, emb), SUM),
            pltpu.VMEM((towers - 1, pad, emb), SUM),
            pltpu.VMEM((towers - 1, pad, emb), SUM),
            pltpu.VMEM((towers, pad, emb), jnp.bfloat16),
            pltpu.VMEM((planes, pad, emb), jnp.bfloat16),
            pltpu.VMEM((towers, pad, emb), WIRE),
            pltpu.VMEM((planes, pad, emb), WIRE),
            pltpu.VMEM((towers - 1, pad, emb), WIRE),
            pltpu.VMEM((planes - 1, pad, emb), WIRE),
            pltpu.SemaphoreType.DMA((5,)),
        ] + sems,
        compiler_params=pltpu.CompilerParams(collective_id=0, has_side_effects=True),
    )(logit_scale, logit_bias, image_feats, text_tokens, lengths, w_image, w_text)


def solution(mesh):
    shape = dict(mesh.shape)
    planes = shape["loss"] * shape["pipe"]
    return jax.shard_map(
        functools.partial(per_device, shape["tower"], shape["pipe"], planes),
        mesh=mesh,
        in_specs=(
            P("loss", "pipe", None, "tower"),
            P("loss", "pipe", None, None, "tower"),
            P("loss", "pipe", None),
            P("tower", None),
            P("tower", None),
            P(),
            P(),
        ),
        out_specs=(P("loss", "pipe", "tower", None), P("loss", "pipe", "tower", None)),
        check_vma=False,
    )
```

```python
import functools

import jax
import jax.numpy as jnp
from jax import lax
from jax.experimental import pallas as pl
from jax.experimental.pallas import tpu as pltpu
from jax.sharding import PartitionSpec as P

MESH = pl.DeviceIdType.MESH
WIRE = jnp.bfloat16
SUM = jnp.float32
F32 = jnp.float32
UNROLL = 16


def each(lo, hi, body):
    if hi - lo <= UNROLL:
        for k in range(lo, hi):
            body(k)
    else:
        lax.fori_loop(lo, hi, lambda k, c: (body(k), c)[1], 0)


def kernel(
    sub, towers, pipes, planes,
    scale_hbm, shift_hbm, feats_hbm, words_hbm, lens_hbm, wi_hbm, wt_hbm,
    image_out, text_out,
    scale_ref, shift_ref, feats, words, lens, wi, wt,
    part_i, part_t, got_i, got_t, images, texts, term_i, term_t, back_i, back_t,
    load_sem, s1, r1, s2, r2, s3, r3, s4, r4, s5, r5, s6, r6,
):
    pad = images.shape[1]
    group, width = feats.shape
    length = words.shape[1]
    emb = wi.shape[1]
    rows = towers * pad
    tower = lax.axis_index("tower")
    plane = lax.axis_index("loss") * pipes + lax.axis_index("pipe")

    def tower_peer(k):
        return {"tower": lax.rem(tower + k, towers)}

    def plane_peer(k):
        q = lax.rem(plane + k, planes)
        return {"loss": q // pipes, "pipe": lax.rem(q, pipes)}

    loads = []
    for n, (src, dst) in enumerate((
        (lens_hbm.at[0], lens),
        (words_hbm.at[0, 0], words),
        (wt_hbm, wt),
        (feats_hbm.at[0, 0], feats),
        (wi_hbm, wi),
        (scale_hbm, scale_ref),
        (shift_hbm, shift_ref),
    )):
        loads.append(pltpu.make_async_copy(src, dst, load_sem.at[n]))
        loads[-1].start()

    barrier = pltpu.get_barrier_semaphore()
    each(1, towers, lambda k: pl.semaphore_signal(
        barrier, inc=1, device_id=tower_peer(k), device_id_type=MESH))
    each(1, planes, lambda k: pl.semaphore_signal(
        barrier, inc=1, device_id=plane_peer(k), device_id_type=MESH))

    def source_row(shape):
        at = lax.broadcasted_iota(jnp.int32, shape, 0)
        r = at % pad
        return jnp.where(r < sub, at // pad * sub + r, -1)

    pick = (source_row((rows, group)) == lax.broadcasted_iota(jnp.int32, (rows, group), 1))

    def scatter(k, part, got, send, recv):
        return pltpu.make_async_remote_copy(
            src_ref=part.at[lax.rem(tower + k, towers)], dst_ref=got.at[k - 1],
            send_sem=send.at[k - 1], recv_sem=recv.at[k - 1],
            device_id=tower_peer(k), device_id_type=MESH)

    loads[0].wait()
    counts = jnp.sum(jnp.where(pick, lens[...].astype(F32), 0.0), axis=1, keepdims=True)
    spot = lax.broadcasted_iota(jnp.int32, (rows, group * length), 1)
    first = source_row((rows, group * length)) * length
    keep = (spot >= first) & (spot < first + counts.astype(jnp.int32)) & (first >= 0)
    keep = jnp.where(keep, 1.0, 0.0).astype(jnp.bfloat16)
    loads[1].wait()
    summed = jnp.dot(keep, words[...].reshape(group * length, words.shape[2]),
                     preferred_element_type=F32)
    pooled = (summed / jnp.maximum(counts, 1.0)).astype(jnp.bfloat16)
    loads[2].wait()
    raw_t = jnp.dot(pooled, wt[...], preferred_element_type=F32).reshape(towers, pad, emb)
    part_t[...] = raw_t
    pl.semaphore_wait(barrier, towers + planes - 2)
    each(1, towers, lambda k: scatter(k, part_t, got_t, s1, r1).start())

    loads[3].wait()
    moved = jnp.dot(jnp.where(pick, 1.0, 0.0).astype(jnp.bfloat16), feats[...],
                    preferred_element_type=F32).astype(jnp.bfloat16)
    loads[4].wait()
    raw_i = jnp.dot(moved, wi[...], preferred_element_type=F32).reshape(towers, pad, emb)
    part_i[...] = raw_i
    each(1, towers, lambda k: scatter(k, part_i, got_i, s2, r2).start())

    def unit(part, got, send, recv):
        each(1, towers, lambda k: scatter(k, part, got, send, recv).wait_recv())
        raw = part[tower]
        for k in range(towers - 1):
            raw = raw + got[k]
        size = jnp.sum(raw * raw, axis=-1, keepdims=True) + 1e-06
        return (raw * lax.rsqrt(size)).astype(jnp.bfloat16)

    def spread_t(k):
        return pltpu.make_async_remote_copy(
            src_ref=texts.at[plane], dst_ref=texts.at[plane],
            send_sem=s3.at[k - 1], recv_sem=r3.at[k - 1],
            device_id=plane_peer(k), device_id_type=MESH)

    def spread_i(k):
        return pltpu.make_async_remote_copy(
            src_ref=images.at[tower], dst_ref=images.at[tower],
            send_sem=s4.at[k - 1], recv_sem=r4.at[k - 1],
            device_id=tower_peer(k), device_id_type=MESH)

    texts[plane] = unit(part_t, got_t, s1, r1)
    each(1, planes, lambda k: spread_t(k).start())
    images[tower] = unit(part_i, got_i, s2, r2)
    each(1, towers, lambda k: spread_i(k).start())
    each(1, planes, lambda k: spread_t(k).wait_recv())
    each(1, towers, lambda k: spread_i(k).wait_recv())

    loads[5].wait()
    loads[6].wait()
    scale = scale_ref[0]
    shift = shift_ref[0]
    cols = planes * pad
    all_i = images[...].astype(F32).reshape(rows, emb).astype(jnp.bfloat16)
    all_t = texts[...].astype(F32).reshape(cols, emb).astype(jnp.bfloat16)
    scores = lax.dot_general(all_i, all_t, (((1,), (1,)), ((), ())), preferred_element_type=F32)
    at_i = lax.broadcasted_iota(jnp.int32, (rows, cols), 0) - tower * pad
    at_t = lax.broadcasted_iota(jnp.int32, (rows, cols), 1) - plane * pad
    match = jnp.where((at_i == at_t) & (at_i >= 0) & (at_i < pad), 1.0, 0.0)
    grads = jax.nn.sigmoid(scale * scores + shift) - match

    def back_image(k):
        return pltpu.make_async_remote_copy(
            src_ref=term_i.at[lax.rem(tower + k, towers)], dst_ref=back_i.at[k - 1],
            send_sem=s5.at[k - 1], recv_sem=r5.at[k - 1],
            device_id=tower_peer(k), device_id_type=MESH)

    def back_text(k):
        return pltpu.make_async_remote_copy(
            src_ref=term_t.at[lax.rem(plane + k, planes)], dst_ref=back_t.at[k - 1],
            send_sem=s6.at[k - 1], recv_sem=r6.at[k - 1],
            device_id=plane_peer(k), device_id_type=MESH)

    grads_t = grads.T.astype(jnp.bfloat16)
    sums_t = jnp.dot(grads_t, all_i, preferred_element_type=F32)
    term_t[...] = sums_t.reshape(planes, pad, emb).astype(WIRE)
    each(1, planes, lambda k: back_text(k).start())
    sums_i = jnp.dot(grads.astype(jnp.bfloat16), all_t, preferred_element_type=F32)
    term_i[...] = sums_i.reshape(towers, pad, emb).astype(WIRE)
    each(1, towers, lambda k: back_image(k).start())

    mine_t = lax.broadcasted_iota(jnp.int32, (pad, cols), 0) + plane * pad
    mine_t = jnp.where(mine_t == lax.broadcasted_iota(jnp.int32, (pad, cols), 1), 1.0, 0.0)
    mine_i = lax.broadcasted_iota(jnp.int32, (pad, rows), 0) + tower * pad
    mine_i = jnp.where(mine_i == lax.broadcasted_iota(jnp.int32, (pad, rows), 1), 1.0, 0.0)
    own_gt = jnp.dot(mine_t.astype(jnp.bfloat16), grads_t, preferred_element_type=F32)
    own_gi = jnp.dot(mine_i.astype(jnp.bfloat16), grads.astype(jnp.bfloat16),
                     preferred_element_type=F32)
    own_t = jnp.dot(own_gt.astype(jnp.bfloat16), all_i, preferred_element_type=F32)
    own_i = jnp.dot(own_gi.astype(jnp.bfloat16), all_t, preferred_element_type=F32)

    each(1, planes, lambda k: back_text(k).wait_recv())
    text_out[:, 0, :] = (own_t + jnp.sum(back_t[...].astype(F32), axis=0))[:sub]
    each(1, towers, lambda k: back_image(k).wait_recv())
    image_out[:, 0, :] = (own_i + jnp.sum(back_i[...].astype(F32), axis=0))[:sub]

    each(1, towers, lambda k: scatter(k, part_t, got_t, s1, r1).wait_send())
    each(1, towers, lambda k: scatter(k, part_i, got_i, s2, r2).wait_send())
    each(1, planes, lambda k: spread_t(k).wait_send())
    each(1, towers, lambda k: spread_i(k).wait_send())
    each(1, towers, lambda k: back_image(k).wait_send())
    each(1, planes, lambda k: back_text(k).wait_send())


def finish(scale_ref, image_ref, text_ref, image_out, text_out):
    image_out[...] = scale_ref[0] * image_ref[...]
    text_out[...] = scale_ref[0] * text_ref[...]


def per_device(towers, pipes, planes, image_feats, text_tokens, lengths, w_image, w_text,
               logit_scale, logit_bias):
    group = image_feats.shape[2]
    emb = w_image.shape[1]
    sub = group // towers
    pad = sub
    out = jax.ShapeDtypeStruct((sub, 1, emb), F32)
    sems = []
    for n in (towers, towers, planes, towers, towers, planes):
        sems += [pltpu.SemaphoreType.DMA((n - 1,))] * 2
    outs = pl.pallas_call(
        functools.partial(kernel, sub, towers, pipes, planes),
        out_shape=(out, out),
        in_specs=[pl.BlockSpec(memory_space=pltpu.HBM)] * 2
        + [pl.BlockSpec(memory_space=pl.ANY)] * 5,
        out_specs=(pl.BlockSpec(memory_space=pltpu.VMEM),) * 2,
        scratch_shapes=[
            pltpu.SMEM(logit_scale.shape, F32),
            pltpu.SMEM(logit_bias.shape, F32),
            pltpu.VMEM(image_feats.shape[2:], image_feats.dtype),
            pltpu.VMEM(text_tokens.shape[2:], text_tokens.dtype),
            pltpu.VMEM(lengths.shape[1:], lengths.dtype),
            pltpu.VMEM(w_image.shape, w_image.dtype),
            pltpu.VMEM(w_text.shape, w_text.dtype),
            pltpu.VMEM((towers, pad, emb), SUM),
            pltpu.VMEM((towers, pad, emb), SUM),
            pltpu.VMEM((towers - 1, pad, emb), SUM),
            pltpu.VMEM((towers - 1, pad, emb), SUM),
            pltpu.VMEM((towers, pad, emb), jnp.bfloat16),
            pltpu.VMEM((planes, pad, emb), jnp.bfloat16),
            pltpu.VMEM((towers, pad, emb), WIRE),
            pltpu.VMEM((planes, pad, emb), WIRE),
            pltpu.VMEM((towers - 1, pad, emb), WIRE),
            pltpu.VMEM((planes - 1, pad, emb), WIRE),
            pltpu.SemaphoreType.DMA((7,)),
        ] + sems,
        compiler_params=pltpu.CompilerParams(collective_id=0, has_side_effects=True),
    )(logit_scale, logit_bias, image_feats, text_tokens, lengths, w_image, w_text)
    outs = pl.pallas_call(
        finish,
        out_shape=(out, out),
        in_specs=[pl.BlockSpec(memory_space=pltpu.SMEM)]
        + [pl.BlockSpec(memory_space=pltpu.VMEM)] * 2,
        out_specs=(pl.BlockSpec(memory_space=pltpu.VMEM),) * 2,
    )(logit_scale, *outs)
    return tuple(o.reshape(1, 1, sub, emb) for o in outs)


def solution(mesh):
    shape = dict(mesh.shape)
    planes = shape["loss"] * shape["pipe"]
    return jax.shard_map(
        functools.partial(per_device, shape["tower"], shape["pipe"], planes),
        mesh=mesh,
        in_specs=(
            P("loss", "pipe", None, "tower"),
            P("loss", "pipe", None, None, "tower"),
            P("loss", "pipe", None),
            P("tower", None),
            P("tower", None),
            P(),
            P(),
        ),
        out_specs=(P("loss", "pipe", "tower", None), P("loss", "pipe", "tower", None)),
        check_vma=False,
    )
```

```python
import functools

import jax
import jax.numpy as jnp
from jax import lax
from jax.experimental import pallas as pl
from jax.experimental.pallas import tpu as pltpu
from jax.sharding import PartitionSpec as P

MESH = pl.DeviceIdType.MESH
WIRE = jnp.bfloat16
SUM = jnp.float32
F32 = jnp.float32
UNROLL = 16
LANES = 128


def each(lo, hi, body):
    if hi - lo <= UNROLL:
        for k in range(lo, hi):
            body(k)
    else:
        lax.fori_loop(lo, hi, lambda k, c: (body(k), c)[1], 0)


def kernel(
    sub, towers, pipes, planes,
    scale_hbm, shift_hbm, feats_hbm, words_hbm, lens_hbm, wi_hbm, wt_hbm,
    image_out, text_out,
    scale_ref, shift_ref, feats, words, lens, wi, wt,
    part_i, part_t, got_i, got_t, images, texts, term_i, term_t, back_i, back_t,
    flat, load_sem, s1, r1, s2, r2, s3, r3, s4, r4, s5, r5, s6, r6,
):
    pad = -(-sub // 8) * 8
    group, width = feats.shape
    length = words.shape[1]
    emb = wi.shape[1]
    rows = towers * pad
    tower = lax.axis_index("tower")
    plane = lax.axis_index("loss") * pipes + lax.axis_index("pipe")

    def tower_peer(k):
        return {"tower": lax.rem(tower + k, towers)}

    def plane_peer(k):
        q = lax.rem(plane + k, planes)
        return {"loss": q // pipes, "pipe": lax.rem(q, pipes)}

    loads = []
    for n, (src, dst) in enumerate((
        (lens_hbm.at[0], lens),
        (words_hbm.at[0, 0], words),
        (wt_hbm, wt),
        (feats_hbm.at[0, 0], feats),
        (wi_hbm, wi),
        (scale_hbm, scale_ref),
        (shift_hbm, shift_ref),
    )):
        loads.append(pltpu.make_async_copy(src, dst, load_sem.at[n]))
        loads[-1].start()

    barrier = pltpu.get_barrier_semaphore()
    each(1, towers, lambda k: pl.semaphore_signal(
        barrier, inc=1, device_id=tower_peer(k), device_id_type=MESH))
    each(1, planes, lambda k: pl.semaphore_signal(
        barrier, inc=1, device_id=plane_peer(k), device_id_type=MESH))

    def source_row(shape):
        at = lax.broadcasted_iota(jnp.int32, shape, 0)
        r = at % pad
        return jnp.where(r < sub, at // pad * sub + r, -1)

    pick = (source_row((rows, group)) == lax.broadcasted_iota(jnp.int32, (rows, group), 1))

    def scatter(k, part, got, send, recv):
        return pltpu.make_async_remote_copy(
            src_ref=part.at[lax.rem(tower + k, towers)], dst_ref=got.at[k - 1],
            send_sem=send.at[k - 1], recv_sem=recv.at[k - 1],
            device_id=tower_peer(k), device_id_type=MESH)

    def pack(part, raw):
        for d in range(towers):
            for c in range(emb // LANES):
                part[d, c * sub:(c + 1) * sub, :] = raw[
                    d * pad:d * pad + sub, c * LANES:(c + 1) * LANES]

    loads[0].wait()
    counts = jnp.sum(jnp.where(pick, lens[...].astype(F32), 0.0), axis=1, keepdims=True)
    spot = lax.broadcasted_iota(jnp.int32, (rows, group * length), 1)
    first = source_row((rows, group * length)) * length
    keep = (spot >= first) & (spot < first + counts.astype(jnp.int32)) & (first >= 0)
    keep = jnp.where(keep, 1.0, 0.0).astype(jnp.bfloat16)
    loads[1].wait()
    summed = jnp.dot(keep, words[...].reshape(group * length, words.shape[2]),
                     preferred_element_type=F32)
    pooled = (summed / jnp.maximum(counts, 1.0)).astype(jnp.bfloat16)
    loads[2].wait()
    raw_t = jnp.dot(pooled, wt[...], preferred_element_type=F32)
    pack(part_t, raw_t)
    pl.semaphore_wait(barrier, towers + planes - 2)
    each(1, towers, lambda k: scatter(k, part_t, got_t, s1, r1).start())

    loads[3].wait()
    moved = jnp.dot(jnp.where(pick, 1.0, 0.0).astype(jnp.bfloat16), feats[...],
                    preferred_element_type=F32).astype(jnp.bfloat16)
    loads[4].wait()
    raw_i = jnp.dot(moved, wi[...], preferred_element_type=F32)
    pack(part_i, raw_i)
    each(1, towers, lambda k: scatter(k, part_i, got_i, s2, r2).start())

    def padded(x):
        x = x.astype(F32)
        if pad > sub:
            x = jnp.concatenate([x, jnp.zeros((x.shape[0], pad - sub, emb), F32)], axis=1)
        return x.reshape(x.shape[0] * pad, emb).astype(jnp.bfloat16)

    def unit(part, got, send, recv):
        each(1, towers, lambda k: scatter(k, part, got, send, recv).wait_recv())
        raw = part[tower]
        for k in range(towers - 1):
            raw = raw + got[k]
        flat[...] = raw
        raw = jnp.concatenate(
            [flat[c * sub:(c + 1) * sub, :] for c in range(emb // LANES)], axis=1)
        size = jnp.sum(raw * raw, axis=-1, keepdims=True) + 1e-06
        return (raw * lax.rsqrt(size)).astype(jnp.bfloat16)

    def spread_t(k):
        return pltpu.make_async_remote_copy(
            src_ref=texts.at[plane], dst_ref=texts.at[plane],
            send_sem=s3.at[k - 1], recv_sem=r3.at[k - 1],
            device_id=plane_peer(k), device_id_type=MESH)

    def spread_i(k):
        return pltpu.make_async_remote_copy(
            src_ref=images.at[tower], dst_ref=images.at[tower],
            send_sem=s4.at[k - 1], recv_sem=r4.at[k - 1],
            device_id=tower_peer(k), device_id_type=MESH)

    texts[plane] = unit(part_t, got_t, s1, r1)
    each(1, planes, lambda k: spread_t(k).start())
    images[tower] = unit(part_i, got_i, s2, r2)
    each(1, towers, lambda k: spread_i(k).start())
    each(1, planes, lambda k: spread_t(k).wait_recv())
    each(1, towers, lambda k: spread_i(k).wait_recv())

    loads[5].wait()
    loads[6].wait()
    scale = scale_ref[0]
    shift = shift_ref[0]
    cols = planes * pad
    all_i = padded(images[...])
    all_t = padded(texts[...])
    scores = lax.dot_general(all_i, all_t, (((1,), (1,)), ((), ())), preferred_element_type=F32)
    at_i = lax.broadcasted_iota(jnp.int32, (rows, cols), 0) - tower * pad
    at_t = lax.broadcasted_iota(jnp.int32, (rows, cols), 1) - plane * pad
    match = jnp.where((at_i == at_t) & (at_i >= 0) & (at_i < pad), 1.0, 0.0)
    grads = jax.nn.sigmoid(scale * scores + shift) - match

    def back_image(k):
        return pltpu.make_async_remote_copy(
            src_ref=term_i.at[lax.rem(tower + k, towers)], dst_ref=back_i.at[k - 1],
            send_sem=s5.at[k - 1], recv_sem=r5.at[k - 1],
            device_id=tower_peer(k), device_id_type=MESH)

    def back_text(k):
        return pltpu.make_async_remote_copy(
            src_ref=term_t.at[lax.rem(plane + k, planes)], dst_ref=back_t.at[k - 1],
            send_sem=s6.at[k - 1], recv_sem=r6.at[k - 1],
            device_id=plane_peer(k), device_id_type=MESH)

    grads_t = grads.T.astype(jnp.bfloat16)
    sums_t = jnp.dot(grads_t, all_i, preferred_element_type=F32)
    term_t[...] = sums_t.reshape(planes, pad, emb)[:, :sub].astype(WIRE)
    each(1, planes, lambda k: back_text(k).start())
    sums_i = jnp.dot(grads.astype(jnp.bfloat16), all_t, preferred_element_type=F32)
    term_i[...] = sums_i.reshape(towers, pad, emb)[:, :sub].astype(WIRE)
    each(1, towers, lambda k: back_image(k).start())

    mine_t = lax.broadcasted_iota(jnp.int32, (pad, cols), 0) + plane * pad
    mine_t = jnp.where(mine_t == lax.broadcasted_iota(jnp.int32, (pad, cols), 1), 1.0, 0.0)
    mine_i = lax.broadcasted_iota(jnp.int32, (pad, rows), 0) + tower * pad
    mine_i = jnp.where(mine_i == lax.broadcasted_iota(jnp.int32, (pad, rows), 1), 1.0, 0.0)
    own_gt = jnp.dot(mine_t.astype(jnp.bfloat16), grads_t, preferred_element_type=F32)
    own_gi = jnp.dot(mine_i.astype(jnp.bfloat16), grads.astype(jnp.bfloat16),
                     preferred_element_type=F32)
    own_t = jnp.dot(own_gt.astype(jnp.bfloat16), all_i, preferred_element_type=F32)
    own_i = jnp.dot(own_gi.astype(jnp.bfloat16), all_t, preferred_element_type=F32)

    each(1, planes, lambda k: back_text(k).wait_recv())
    text_out[:, 0, :] = (own_t[:sub] + jnp.sum(back_t[...].astype(F32), axis=0))
    each(1, towers, lambda k: back_image(k).wait_recv())
    image_out[:, 0, :] = (own_i[:sub] + jnp.sum(back_i[...].astype(F32), axis=0))

    each(1, towers, lambda k: scatter(k, part_t, got_t, s1, r1).wait_send())
    each(1, towers, lambda k: scatter(k, part_i, got_i, s2, r2).wait_send())
    each(1, planes, lambda k: spread_t(k).wait_send())
    each(1, towers, lambda k: spread_i(k).wait_send())
    each(1, towers, lambda k: back_image(k).wait_send())
    each(1, planes, lambda k: back_text(k).wait_send())


def finish(scale_ref, image_ref, text_ref, image_out, text_out):
    image_out[...] = scale_ref[0] * image_ref[...]
    text_out[...] = scale_ref[0] * text_ref[...]


def per_device(towers, pipes, planes, image_feats, text_tokens, lengths, w_image, w_text,
               logit_scale, logit_bias):
    group = image_feats.shape[2]
    emb = w_image.shape[1]
    sub = group // towers
    out = jax.ShapeDtypeStruct((sub, 1, emb), F32)
    sems = []
    for n in (towers, towers, planes, towers, towers, planes):
        sems += [pltpu.SemaphoreType.DMA((n - 1,))] * 2
    outs = pl.pallas_call(
        functools.partial(kernel, sub, towers, pipes, planes),
        out_shape=(out, out),
        in_specs=[pl.BlockSpec(memory_space=pltpu.HBM)] * 2
        + [pl.BlockSpec(memory_space=pl.ANY)] * 5,
        out_specs=(pl.BlockSpec(memory_space=pltpu.VMEM),) * 2,
        scratch_shapes=[
            pltpu.SMEM(logit_scale.shape, F32),
            pltpu.SMEM(logit_bias.shape, F32),
            pltpu.VMEM(image_feats.shape[2:], image_feats.dtype),
            pltpu.VMEM(text_tokens.shape[2:], text_tokens.dtype),
            pltpu.VMEM(lengths.shape[1:], lengths.dtype),
            pltpu.VMEM(w_image.shape, w_image.dtype),
            pltpu.VMEM(w_text.shape, w_text.dtype),
            pltpu.VMEM((towers, sub * emb // LANES, LANES), SUM),
            pltpu.VMEM((towers, sub * emb // LANES, LANES), SUM),
            pltpu.VMEM((towers - 1, sub * emb // LANES, LANES), SUM),
            pltpu.VMEM((towers - 1, sub * emb // LANES, LANES), SUM),
            pltpu.VMEM((towers, sub, emb), jnp.bfloat16),
            pltpu.VMEM((planes, sub, emb), jnp.bfloat16),
            pltpu.VMEM((towers, sub, emb), WIRE),
            pltpu.VMEM((planes, sub, emb), WIRE),
            pltpu.VMEM((towers - 1, sub, emb), WIRE),
            pltpu.VMEM((planes - 1, sub, emb), WIRE),
            pltpu.VMEM((sub * emb // LANES, LANES), SUM),
            pltpu.SemaphoreType.DMA((7,)),
        ] + sems,
        compiler_params=pltpu.CompilerParams(collective_id=0, has_side_effects=True),
    )(logit_scale, logit_bias, image_feats, text_tokens, lengths, w_image, w_text)
    outs = pl.pallas_call(
        finish,
        out_shape=(out, out),
        in_specs=[pl.BlockSpec(memory_space=pltpu.SMEM)]
        + [pl.BlockSpec(memory_space=pltpu.VMEM)] * 2,
        out_specs=(pl.BlockSpec(memory_space=pltpu.VMEM),) * 2,
    )(logit_scale, *outs)
    return tuple(o.reshape(1, 1, sub, emb) for o in outs)


def solution(mesh):
    shape = dict(mesh.shape)
    planes = shape["loss"] * shape["pipe"]
    return jax.shard_map(
        functools.partial(per_device, shape["tower"], shape["pipe"], planes),
        mesh=mesh,
        in_specs=(
            P("loss", "pipe", None, "tower"),
            P("loss", "pipe", None, None, "tower"),
            P("loss", "pipe", None),
            P("tower", None),
            P("tower", None),
            P(),
            P(),
        ),
        out_specs=(P("loss", "pipe", "tower", None), P("loss", "pipe", "tower", None)),
        check_vma=False,
    )
```

```python
import functools

import jax
import jax.numpy as jnp
from jax import lax
from jax.experimental import pallas as pl
from jax.experimental.pallas import tpu as pltpu
from jax.sharding import PartitionSpec as P

MESH = pl.DeviceIdType.MESH
WIRE = jnp.bfloat16
SUM = jnp.float32
F32 = jnp.float32
UNROLL = 16
LANES = 128


def each(lo, hi, body):
    if hi - lo <= UNROLL:
        for k in range(lo, hi):
            body(k)
    else:
        lax.fori_loop(lo, hi, lambda k, c: (body(k), c)[1], 0)


def kernel(
    sub, towers, pipes, planes,
    scale_hbm, shift_hbm, feats_hbm, words_hbm, lens_hbm, wi_hbm, wt_hbm,
    image_out, text_out,
    scale_ref, shift_ref, feats, words, lens, wi, wt,
    part_i, part_t, got_i, got_t, images, texts, term_i, term_t, back_i, back_t,
    flat, load_sem, s1, r1, s2, r2, s3, r3, s4, r4, s5, r5, s6, r6,
):
    pad = -(-sub // 8) * 8
    group, width = feats.shape
    length = words.shape[1]
    emb = wi.shape[1]
    rows = towers * pad
    tower = lax.axis_index("tower")
    plane = lax.axis_index("loss") * pipes + lax.axis_index("pipe")

    def tower_peer(k):
        return {"tower": lax.rem(tower + k, towers)}

    def plane_peer(k):
        q = lax.rem(plane + k, planes)
        return {"loss": q // pipes, "pipe": lax.rem(q, pipes)}

    loads = []
    for n, (src, dst) in enumerate((
        (lens_hbm.at[0], lens),
        (words_hbm.at[0, 0], words),
        (wt_hbm, wt),
        (feats_hbm.at[0, 0], feats),
        (wi_hbm, wi),
        (scale_hbm, scale_ref),
        (shift_hbm, shift_ref),
    )):
        loads.append(pltpu.make_async_copy(src, dst, load_sem.at[n]))
        loads[-1].start()

    barrier = pltpu.get_barrier_semaphore()
    each(1, towers, lambda k: pl.semaphore_signal(
        barrier, inc=1, device_id=tower_peer(k), device_id_type=MESH))
    each(1, planes, lambda k: pl.semaphore_signal(
        barrier, inc=1, device_id=plane_peer(k), device_id_type=MESH))

    def source_row(shape):
        at = lax.broadcasted_iota(jnp.int32, shape, 0)
        r = at % pad
        return jnp.where(r < sub, at // pad * sub + r, -1)

    pick = (source_row((rows, group)) == lax.broadcasted_iota(jnp.int32, (rows, group), 1))

    def scatter(k, part, got, send, recv):
        return pltpu.make_async_remote_copy(
            src_ref=part.at[lax.rem(tower + k, towers)], dst_ref=got.at[k - 1],
            send_sem=send.at[k - 1], recv_sem=recv.at[k - 1],
            device_id=tower_peer(k), device_id_type=MESH)

    def pack(part, raw):
        for d in range(towers):
            for c in range(emb // LANES):
                part[d, c * sub:(c + 1) * sub, :] = raw[
                    d * pad:d * pad + sub, c * LANES:(c + 1) * LANES]

    loads[0].wait()
    counts = jnp.sum(jnp.where(pick, lens[...].astype(F32), 0.0), axis=1, keepdims=True)
    spot = lax.broadcasted_iota(jnp.int32, (rows, group * length), 1)
    first = source_row((rows, group * length)) * length
    keep = (spot >= first) & (spot < first + counts.astype(jnp.int32)) & (first >= 0)
    keep = jnp.where(keep, 1.0, 0.0).astype(jnp.bfloat16)
    loads[1].wait()
    summed = jnp.dot(keep, words[...].reshape(group * length, words.shape[2]),
                     preferred_element_type=F32)
    pooled = (summed / jnp.maximum(counts, 1.0)).astype(jnp.bfloat16)
    loads[2].wait()
    raw_t = jnp.dot(pooled, wt[...], preferred_element_type=F32)
    pack(part_t, raw_t)
    pl.semaphore_wait(barrier, towers + planes - 2)
    each(1, towers, lambda k: scatter(k, part_t, got_t, s1, r1).start())

    loads[3].wait()
    moved = jnp.dot(jnp.where(pick, 1.0, 0.0).astype(jnp.bfloat16), feats[...],
                    preferred_element_type=F32).astype(jnp.bfloat16)
    loads[4].wait()
    raw_i = jnp.dot(moved, wi[...], preferred_element_type=F32)
    pack(part_i, raw_i)
    each(1, towers, lambda k: scatter(k, part_i, got_i, s2, r2).start())

    def padded(x):
        x = x.astype(F32)
        if pad > sub:
            x = jnp.concatenate([x, jnp.zeros((x.shape[0], pad - sub, emb), F32)], axis=1)
        return x.reshape(x.shape[0] * pad, emb).astype(jnp.bfloat16)

    def unit(part, got, send, recv):
        each(1, towers, lambda k: scatter(k, part, got, send, recv).wait_recv())
        raw = part[tower]
        for k in range(towers - 1):
            raw = raw + got[k]
        flat[...] = raw
        raw = jnp.concatenate(
            [flat[c * sub:(c + 1) * sub, :] for c in range(emb // LANES)], axis=1)
        size = jnp.sum(raw * raw, axis=-1, keepdims=True) + 1e-06
        return (raw * lax.rsqrt(size)).astype(jnp.bfloat16)

    def spread_t(k):
        return pltpu.make_async_remote_copy(
            src_ref=texts.at[plane], dst_ref=texts.at[plane],
            send_sem=s3.at[k - 1], recv_sem=r3.at[k - 1],
            device_id=plane_peer(k), device_id_type=MESH)

    def spread_i(k):
        return pltpu.make_async_remote_copy(
            src_ref=images.at[tower], dst_ref=images.at[tower],
            send_sem=s4.at[k - 1], recv_sem=r4.at[k - 1],
            device_id=tower_peer(k), device_id_type=MESH)

    texts[plane] = unit(part_t, got_t, s1, r1)
    each(1, planes, lambda k: spread_t(k).start())
    images[tower] = unit(part_i, got_i, s2, r2)
    each(1, towers, lambda k: spread_i(k).start())
    each(1, planes, lambda k: spread_t(k).wait_recv())
    each(1, towers, lambda k: spread_i(k).wait_recv())

    loads[5].wait()
    loads[6].wait()
    scale = scale_ref[0]
    shift = shift_ref[0]
    cols = planes * pad
    all_i = padded(images[...])
    all_t = padded(texts[...])
    scores = lax.dot_general(all_i, all_t, (((1,), (1,)), ((), ())), preferred_element_type=F32)
    at_i = lax.broadcasted_iota(jnp.int32, (rows, cols), 0) - tower * pad
    at_t = lax.broadcasted_iota(jnp.int32, (rows, cols), 1) - plane * pad
    match = jnp.where((at_i == at_t) & (at_i >= 0) & (at_i < pad), 1.0, 0.0)
    grads = jax.nn.sigmoid(scale * scores + shift) - match

    def back_image(k):
        return pltpu.make_async_remote_copy(
            src_ref=term_i.at[lax.rem(tower + k, towers)], dst_ref=back_i.at[k - 1],
            send_sem=s5.at[k - 1], recv_sem=r5.at[k - 1],
            device_id=tower_peer(k), device_id_type=MESH)

    def back_text(k):
        return pltpu.make_async_remote_copy(
            src_ref=term_t.at[lax.rem(plane + k, planes)], dst_ref=back_t.at[k - 1],
            send_sem=s6.at[k - 1], recv_sem=r6.at[k - 1],
            device_id=plane_peer(k), device_id_type=MESH)

    sums_i = jnp.dot(grads.astype(jnp.bfloat16), all_t, preferred_element_type=F32)
    term_i[...] = sums_i.reshape(towers, pad, emb)[:, :sub].astype(WIRE)
    each(1, towers, lambda k: back_image(k).start())
    grads_t = grads.T.astype(jnp.bfloat16)
    sums_t = jnp.dot(grads_t, all_i, preferred_element_type=F32)
    term_t[...] = sums_t.reshape(planes, pad, emb)[:, :sub].astype(WIRE)
    each(1, planes, lambda k: back_text(k).start())

    mine_t = lax.broadcasted_iota(jnp.int32, (pad, cols), 0) + plane * pad
    mine_t = jnp.where(mine_t == lax.broadcasted_iota(jnp.int32, (pad, cols), 1), 1.0, 0.0)
    mine_i = lax.broadcasted_iota(jnp.int32, (pad, rows), 0) + tower * pad
    mine_i = jnp.where(mine_i == lax.broadcasted_iota(jnp.int32, (pad, rows), 1), 1.0, 0.0)
    own_gt = jnp.dot(mine_t.astype(jnp.bfloat16), grads_t, preferred_element_type=F32)
    own_gi = jnp.dot(mine_i.astype(jnp.bfloat16), grads.astype(jnp.bfloat16),
                     preferred_element_type=F32)
    own_t = jnp.dot(own_gt.astype(jnp.bfloat16), all_i, preferred_element_type=F32)
    own_i = jnp.dot(own_gi.astype(jnp.bfloat16), all_t, preferred_element_type=F32)

    each(1, planes, lambda k: back_text(k).wait_recv())
    text_out[:, 0, :] = (own_t[:sub] + jnp.sum(back_t[...].astype(F32), axis=0))
    each(1, towers, lambda k: back_image(k).wait_recv())
    image_out[:, 0, :] = (own_i[:sub] + jnp.sum(back_i[...].astype(F32), axis=0))

    each(1, towers, lambda k: scatter(k, part_t, got_t, s1, r1).wait_send())
    each(1, towers, lambda k: scatter(k, part_i, got_i, s2, r2).wait_send())
    each(1, planes, lambda k: spread_t(k).wait_send())
    each(1, towers, lambda k: spread_i(k).wait_send())
    each(1, towers, lambda k: back_image(k).wait_send())
    each(1, planes, lambda k: back_text(k).wait_send())


def finish(scale_ref, image_ref, text_ref, image_out, text_out):
    image_out[...] = scale_ref[0] * image_ref[...]
    text_out[...] = scale_ref[0] * text_ref[...]


def per_device(towers, pipes, planes, image_feats, text_tokens, lengths, w_image, w_text,
               logit_scale, logit_bias):
    group = image_feats.shape[2]
    emb = w_image.shape[1]
    sub = group // towers
    out = jax.ShapeDtypeStruct((sub, 1, emb), F32)
    sems = []
    for n in (towers, towers, planes, towers, towers, planes):
        sems += [pltpu.SemaphoreType.DMA((n - 1,))] * 2
    outs = pl.pallas_call(
        functools.partial(kernel, sub, towers, pipes, planes),
        out_shape=(out, out),
        in_specs=[pl.BlockSpec(memory_space=pltpu.HBM)] * 2
        + [pl.BlockSpec(memory_space=pl.ANY)] * 5,
        out_specs=(pl.BlockSpec(memory_space=pltpu.VMEM),) * 2,
        scratch_shapes=[
            pltpu.SMEM(logit_scale.shape, F32),
            pltpu.SMEM(logit_bias.shape, F32),
            pltpu.VMEM(image_feats.shape[2:], image_feats.dtype),
            pltpu.VMEM(text_tokens.shape[2:], text_tokens.dtype),
            pltpu.VMEM(lengths.shape[1:], lengths.dtype),
            pltpu.VMEM(w_image.shape, w_image.dtype),
            pltpu.VMEM(w_text.shape, w_text.dtype),
            pltpu.VMEM((towers, sub * emb // LANES, LANES), SUM),
            pltpu.VMEM((towers, sub * emb // LANES, LANES), SUM),
            pltpu.VMEM((towers - 1, sub * emb // LANES, LANES), SUM),
            pltpu.VMEM((towers - 1, sub * emb // LANES, LANES), SUM),
            pltpu.VMEM((towers, sub, emb), jnp.bfloat16),
            pltpu.VMEM((planes, sub, emb), jnp.bfloat16),
            pltpu.VMEM((towers, sub, emb), WIRE),
            pltpu.VMEM((planes, sub, emb), WIRE),
            pltpu.VMEM((towers - 1, sub, emb), WIRE),
            pltpu.VMEM((planes - 1, sub, emb), WIRE),
            pltpu.VMEM((sub * emb // LANES, LANES), SUM),
            pltpu.SemaphoreType.DMA((7,)),
        ] + sems,
        compiler_params=pltpu.CompilerParams(collective_id=0, has_side_effects=True),
    )(logit_scale, logit_bias, image_feats, text_tokens, lengths, w_image, w_text)
    outs = pl.pallas_call(
        finish,
        out_shape=(out, out),
        in_specs=[pl.BlockSpec(memory_space=pltpu.SMEM)]
        + [pl.BlockSpec(memory_space=pltpu.VMEM)] * 2,
        out_specs=(pl.BlockSpec(memory_space=pltpu.VMEM),) * 2,
    )(logit_scale, *outs)
    return tuple(o.reshape(1, 1, sub, emb) for o in outs)


def solution(mesh):
    shape = dict(mesh.shape)
    planes = shape["loss"] * shape["pipe"]
    return jax.shard_map(
        functools.partial(per_device, shape["tower"], shape["pipe"], planes),
        mesh=mesh,
        in_specs=(
            P("loss", "pipe", None, "tower"),
            P("loss", "pipe", None, None, "tower"),
            P("loss", "pipe", None),
            P("tower", None),
            P("tower", None),
            P(),
            P(),
        ),
        out_specs=(P("loss", "pipe", "tower", None), P("loss", "pipe", "tower", None)),
        check_vma=False,
    )
```
